32 devices in a mesh: roll: 4 (over y, x), seq: 8 (over z, core).
Axes of the slice: x: 2, y: 2, z: 4, core: 2. Of those that a mesh axis runs over, the one named last changes fastest.
Arguments:
- query_rows: bfloat16 [4, 4096, 1792], P('roll', 'seq'), may hold values from -200 to 200
- key_rows: bfloat16 [4, 4096, 256], P('roll', 'seq'), may hold values from -6 to 6
- value_rows: bfloat16 [4, 4096, 256], P('roll', 'seq'), may hold values from -6 to 6
- cotangent: bfloat16 [4, 4096, 1792], P('roll', None, 'seq'), may hold values from -6 to 6
- slopes: float32 [14], replicated, may hold values from 0.00029296876 to 0.0390625
- lengths: int32 [4], P('roll'), may hold values from 1024 to 4096, as said below
- loss_mask: int32 [4, 4096], P('roll', 'seq'), may hold values 0 or 1
- distances: int32 [4], P('roll'), may hold values from 40 to 357
Outputs:
- grad_queries: bfloat16 [4, 4096, 1792], P('roll', 'seq')
- grad_keys: bfloat16 [4, 4096, 256], P('roll', 'seq')
- grad_values: bfloat16 [4, 4096, 256], P('roll', 'seq')
The draws below stay inside these ranges and needn't reach their ends.
Inputs may be any that keep to these rules, and one draw needn't show every extreme that they name: `lengths`: some rollout has 4096 tokens and some 4096 // 4.
All inputs are finite; a program needn't handle non-finite values. No bound on the sum of `loss_mask` on one device may be relied on, other than what follows from the above.
Results may differ from the reference program's by a relative error of at most 0.0068.
Values may be sent and summed in bfloat16 or wider, within the bound.
No kernel may reach another device: no remote copies, remote signals or barrier semaphores. Data moves between devices by JAX's collectives and lax.ppermute only.
A program may use at most 64 MiB of HBM per device.

```python
import math
import jax
import jax.numpy as jnp
from jax import lax

HEADS = 14
KV_HEADS = 2
HEAD_DIM = 128
WINDOW = 1024
TOK_DEV = 512
GROUP = 7
FEAT = 1792
KV_WIDTH = 256
SEQ_LEN = 4096
ROLLS = 4
REACH = 2
N_SEQ = 8


def drawn_pair(key):
    key_base = jnp.clip(jax.random.normal(jax.random.fold_in(key, 11), (ROLLS, SEQ_LEN, KV_WIDTH), jnp.float32), -6.0, 6.0)
    query_base = jnp.clip(jax.random.normal(jax.random.fold_in(key, 12), (ROLLS, SEQ_LEN, FEAT), jnp.float32), -6.0, 6.0)
    return (query_base, key_base)


def draw_query_rows(key, part):
    return drawn_pair(key)[0].astype(jnp.bfloat16)


def draw_key_rows(key, part):
    return drawn_pair(key)[1].astype(jnp.bfloat16)


def draw_lengths(key, part):
    base_len = jax.random.randint(jax.random.fold_in(key, 21), (ROLLS,), SEQ_LEN // 4, SEQ_LEN + 1)
    order = jax.random.permutation(jax.random.fold_in(key, 22), ROLLS)
    base_len = base_len.at[order[0]].set(SEQ_LEN)
    base_len = base_len.at[order[1]].set(SEQ_LEN // 4)
    return base_len.astype(jnp.int32)


def draw_distances(key, part):
    base_dist = jax.random.randint(jax.random.fold_in(key, 31), (ROLLS,), 40, 120)
    base_dist = base_dist.at[0].set(40)
    base_dist = base_dist.at[ROLLS - 1].set(119)
    factor = ROLLS - 1 + 2 * jnp.arange(ROLLS, dtype=jnp.int32)
    return (base_dist * factor // (ROLLS - 1)).astype(jnp.int32)


def place_ends(drawn, key, least, high):
    longest = drawn.shape.index(max(drawn.shape))
    spots = []
    for shift in (0, 1):
        where = [jax.random.randint(jax.random.fold_in(key, axis), (), 0, length) for axis, length in enumerate(drawn.shape)]
        where[longest] = (where[longest] + shift) % drawn.shape[longest]
        spots.append(tuple(where))
    return drawn.at[spots[0]].set(least).at[spots[1]].set(high)


def block_scale(stream_key, shape, cuts, least, top_value):
    factor_of, own = 1.0, jax.random.fold_in(stream_key, 6)
    for axis_at, shards_of in cuts:
        steps = jnp.exp(jax.random.uniform(jax.random.fold_in(own, axis_at), (shards_of,), jnp.float32, least / len(cuts), top_value / len(cuts)))
        factor_of = factor_of * jnp.repeat(steps, shape[axis_at] // shards_of).reshape([-1 if axis == axis_at else 1 for axis in range(len(shape))])
    return factor_of


def scatter_about(key, extent, deviation, limit, shards=(), held_as=jnp.bfloat16):
    gain = block_scale(key, extent, shards, -0.22, 0.18) if shards else 1.0
    result = jax.random.normal(key, extent, jnp.float32) * deviation * gain
    return jnp.minimum(jnp.maximum(result, -limit), limit).astype(held_as)


def setup_inputs(seed: int = 0) -> dict:
    arg_keys = jax.random.split(jax.random.key(seed), 9)
    query_rows = draw_query_rows(jax.random.fold_in(arg_keys[8], 71), 0)
    key_rows = draw_key_rows(jax.random.fold_in(arg_keys[8], 71), 0)
    value_rows = scatter_about(arg_keys[2], (ROLLS, SEQ_LEN, KV_WIDTH), 1.0, 6.0, ((0, 4), (1, 8)))
    cotangent = scatter_about(arg_keys[3], (ROLLS, SEQ_LEN, FEAT), 1.0, 6.0, ((0, 4), (2, 8)))
    slopes = jnp.clip(jnp.exp(jax.random.uniform(arg_keys[4], (HEADS,), jnp.float32, math.log(0.00029296876), math.log(0.0390625))), 0.00029296876, 0.0390625)
    lengths = draw_lengths(jax.random.fold_in(arg_keys[8], 71), 0)
    loss_mask = place_ends((jax.random.randint(arg_keys[6], (ROLLS, SEQ_LEN), 0, 4) < 3).astype(jnp.int32), jax.random.fold_in(arg_keys[6], 1), 0, 1)
    distances = draw_distances(jax.random.fold_in(arg_keys[8], 71), 0)
    return {"query_rows": query_rows, "key_rows": key_rows, "value_rows": value_rows, "cotangent": cotangent, "slopes": slopes, "lengths": lengths, "loss_mask": loss_mask, "distances": distances}


def shard_terms(query_blk, key_band, value_band, dout_blk, slopes, shard_pos):
    attn_scale = 1.0 / math.sqrt(HEAD_DIM)
    band_len = (REACH + 1) * TOK_DEV
    q_heads = query_blk.astype(jnp.float32).reshape(TOK_DEV, KV_HEADS, GROUP, HEAD_DIM)
    k_heads = key_band.astype(jnp.float32).reshape(band_len, KV_HEADS, HEAD_DIM)
    v_heads = value_band.astype(jnp.float32).reshape(band_len, KV_HEADS, HEAD_DIM)
    d_heads = dout_blk.astype(jnp.float32).reshape(TOK_DEV, KV_HEADS, GROUP, HEAD_DIM)
    query_pos = shard_pos * TOK_DEV + jnp.arange(TOK_DEV, dtype=jnp.int32)
    key_pos = (shard_pos - REACH) * TOK_DEV + jnp.arange(band_len, dtype=jnp.int32)
    pos_gap = query_pos[:, None] - key_pos[None, :]
    allowed = (pos_gap >= 0) & (pos_gap < WINDOW) & (key_pos[None, :] >= 0)
    raw = jnp.einsum('igke,jge->gkij', q_heads, k_heads).reshape(HEADS, TOK_DEV, band_len)
    scores = raw * attn_scale - slopes[:, None, None] * pos_gap.astype(jnp.float32)[None]
    masked = jnp.where(allowed[None], scores, -jnp.inf)
    row_max = lax.optimization_barrier(jnp.max(masked, axis=2, keepdims=True))
    exp_terms = jnp.where(allowed[None], jnp.exp(masked - row_max), 0.0)
    probs = exp_terms / lax.optimization_barrier(jnp.sum(exp_terms, axis=2, keepdims=True))
    probs_low = probs.astype(jnp.bfloat16)
    dprob = jnp.einsum('igke,jge->gkij', d_heads, v_heads).reshape(HEADS, TOK_DEV, band_len)
    row_delta = lax.optimization_barrier(jnp.sum(probs * dprob, axis=2, keepdims=True))
    dscore = (probs * (dprob - row_delta) * attn_scale).astype(jnp.bfloat16)
    dscore_wide = dscore.astype(jnp.float32).reshape(KV_HEADS, GROUP, TOK_DEV, band_len)
    probs_wide = probs_low.astype(jnp.float32).reshape(KV_HEADS, GROUP, TOK_DEV, band_len)
    grad_q = jnp.einsum('gkij,jge->igke', dscore_wide, k_heads).reshape(TOK_DEV, FEAT).astype(jnp.bfloat16)
    band_dk = jnp.einsum('gkij,igke->jge', dscore_wide, q_heads).reshape(band_len, KV_WIDTH)
    band_dv = jnp.einsum('gkij,igke->jge', probs_wide, d_heads).reshape(band_len, KV_WIDTH)
    split_at = REACH * TOK_DEV
    part_k = band_dk[:split_at].reshape(REACH, TOK_DEV, KV_WIDTH).astype(jnp.bfloat16)
    part_v = band_dv[:split_at].reshape(REACH, TOK_DEV, KV_WIDTH).astype(jnp.bfloat16)
    return (grad_q, band_dk[split_at:], band_dv[split_at:], part_k, part_v)

def reference(query_rows, key_rows, value_rows, cotangent, slopes, lengths, loss_mask, distances):
    positions = jnp.arange(SEQ_LEN, dtype=jnp.int32)
    valid = ((positions[None, :] < lengths[:, None]) & (loss_mask == 1)).astype(jnp.float32)
    count = lax.optimization_barrier(jnp.sum(valid, axis=1))
    dist_float = distances.astype(jnp.float32)
    advantage = (jnp.sum(dist_float) / ROLLS - dist_float) / 64.0
    weight = advantage[:, None] * valid * SEQ_LEN / (1.0 + count[:, None])
    dout = (cotangent.astype(jnp.float32) * weight[:, :, None]).astype(jnp.bfloat16)

    def one_rollout(inputs):
        q_roll, k_roll, v_roll, d_roll = inputs
        pad_rows = REACH * TOK_DEV
        k_pad = jnp.concatenate([jnp.zeros((pad_rows, KV_WIDTH), k_roll.dtype), k_roll], 0)
        v_pad = jnp.concatenate([jnp.zeros((pad_rows, KV_WIDTH), v_roll.dtype), v_roll], 0)

        def one_shard(shard_pos):
            start = shard_pos * TOK_DEV
            band_len = (REACH + 1) * TOK_DEV
            return shard_terms(lax.dynamic_slice_in_dim(q_roll, start, TOK_DEV), lax.dynamic_slice_in_dim(k_pad, start, band_len), lax.dynamic_slice_in_dim(v_pad, start, band_len), lax.dynamic_slice_in_dim(d_roll, start, TOK_DEV), slopes, shard_pos)
        grad_q, own_k, own_v, part_k, part_v = lax.map(one_shard, jnp.arange(N_SEQ, dtype=jnp.int32))
        total_k = own_k
        total_v = own_v
        for offset in range(1, REACH + 1):
            filler = jnp.zeros((offset, TOK_DEV, KV_WIDTH), part_k.dtype)
            total_k = total_k + jnp.concatenate([part_k[offset:, REACH - offset], filler], 0).astype(jnp.float32)
            total_v = total_v + jnp.concatenate([part_v[offset:, REACH - offset], filler], 0).astype(jnp.float32)
        return (grad_q.reshape(SEQ_LEN, FEAT), total_k.astype(jnp.bfloat16).reshape(SEQ_LEN, KV_WIDTH), total_v.astype(jnp.bfloat16).reshape(SEQ_LEN, KV_WIDTH))
    grad_queries, grad_keys, grad_values = lax.map(one_rollout, (query_rows, key_rows, value_rows, dout))
    return (grad_queries, grad_keys, grad_values)
```

```python
import functools
import math

import jax
import jax.numpy as jnp
from jax import lax
from jax.experimental import pallas as pl
from jax.experimental.pallas import tpu as pltpu
from jax.sharding import PartitionSpec as P

HEAD_DIM = 128
WINDOW = 1024
TILE = 128
FAR = -1e30
LOG2E = math.log2(math.e)


def passed_along(value, axis, steps):
    count = lax.axis_size(axis)
    leading, last = (max(0, -steps), min(count, count - steps))
    return lax.ppermute(value, axis, [(source, source + steps) for source in range(leading, last)])


def flip_kernel(x_ref, out_ref):
    out_ref[...] = x_ref[...].astype(jnp.float32).T.astype(out_ref.dtype)


def flip_blocks(x, rows):
    total, width = x.shape
    count = total // rows
    return pl.pallas_call(
        flip_kernel,
        grid=(count,),
        in_specs=[pl.BlockSpec((rows, width), lambda i: (i, 0))],
        out_specs=pl.BlockSpec((None, width, rows), lambda i: (i, 0, 0)),
        out_shape=jax.ShapeDtypeStruct((count, width, rows), x.dtype),
        name="flip_blocks",
    )(x)


def prob_kernel(group, key_tiles, invalid_ref, slope_ref, qt_ref, k_refs, v_refs, e_ref, o_ref,
                kband, vtband, bias, scores):
    kv_head = pl.program_id(0)
    sub = pl.program_id(1)
    lanes = group * TILE
    blk_rows = k_refs[0].shape[0]
    slope_row = jnp.concatenate(
        [jnp.full((1, TILE), slope_ref[kv_head * group + h] * LOG2E, jnp.float32) for h in range(group)], 1)

    @pl.when(sub == 0)
    def _():
        for n, (k_ref, v_ref) in enumerate(zip(k_refs, v_refs)):
            kband[n * blk_rows:(n + 1) * blk_rows] = k_ref[...]
            vtband[:HEAD_DIM, n * blk_rows:(n + 1) * blk_rows] = (
                v_ref[...].astype(jnp.float32).T.astype(vtband.dtype))
        vtband[HEAD_DIM:] = jnp.ones(vtband[HEAD_DIM:].shape, vtband.dtype)
        bias[...] = lax.broadcasted_iota(jnp.int32, (TILE, lanes), 0).astype(jnp.float32) * slope_row

    scale = LOG2E / math.sqrt(HEAD_DIM)
    qt = jnp.concatenate([qt_ref[h * HEAD_DIM:(h + 1) * HEAD_DIM] for h in range(group)], 1)
    below = (lax.broadcasted_iota(jnp.int32, (TILE, lanes), 0)
             > lax.broadcasted_iota(jnp.int32, (TILE, lanes), 1) % TILE)
    invalid = invalid_ref[0]
    start = pl.multiple_of(sub * TILE, TILE)
    peak = None
    shifts = []
    for t in range(key_tiles):
        k_tile = kband[pl.ds(start + t * TILE, TILE)]
        s = jnp.dot(k_tile, qt, preferred_element_type=jnp.float32) * scale + bias[...]
        if t == 0:
            s = jnp.where(below, s, FAR)
        elif t == key_tiles - 1:
            s = jnp.where(below, FAR, s)
        scores[t * TILE:(t + 1) * TILE] = s
        shift = slope_row * (t * TILE) + jnp.where(sub + t < invalid, FAR, 0.0)
        shifts.append(shift)
        top = jnp.max(s.reshape(TILE // 8, 8, lanes), 0) + shift
        peak = top if peak is None else jnp.maximum(peak, top)
    peak = jnp.max(peak, 0, keepdims=True)
    for t in range(key_tiles):
        e = jnp.exp2(scores[t * TILE:(t + 1) * TILE] - (peak - shifts[t]))
        e_ref[t * TILE:(t + 1) * TILE] = e.astype(e_ref.dtype)
    o_ref[...] = jnp.dot(vtband[:, pl.ds(start, key_tiles * TILE)], e_ref[...],
                         preferred_element_type=jnp.float32)


def grad_kernel(group, key_tiles, scale_ref, keep_ref, dt_ref, qt_ref, k_refs, v_refs, e_ref, o_ref,
                dq_ref, dk_far, dv_far, dk_own, dv_own, kband, ktband, vband, dk_acc, dv_acc, ds_all):
    sub = pl.program_id(1)
    blk_rows = k_refs[0].shape[0]
    lanes = group * TILE

    @pl.when(sub == 0)
    def _():
        for n, (k_ref, v_ref) in enumerate(zip(k_refs, v_refs)):
            rows = slice(n * blk_rows, (n + 1) * blk_rows)
            ktband[:, rows] = k_ref[...].astype(jnp.float32).T.astype(ktband.dtype)
            vband[rows] = v_ref[...]
        dk_acc[...] = jnp.zeros(dk_acc.shape, dk_acc.dtype)
        dv_acc[...] = jnp.zeros(dv_acc.shape, dv_acc.dtype)

    start = pl.multiple_of(sub * TILE, TILE)
    keep = jnp.concatenate([keep_ref[...]] * group, 1)
    inv = 1.0 / o_ref[HEAD_DIM:HEAD_DIM + 1]
    dt = jnp.concatenate([dt_ref[h * HEAD_DIM:(h + 1) * HEAD_DIM] for h in range(group)], 1)
    dt = (dt.astype(jnp.float32) * (keep * inv)).astype(jnp.bfloat16)
    qt = jnp.concatenate([qt_ref[h * HEAD_DIM:(h + 1) * HEAD_DIM] for h in range(group)], 1)
    delta = jnp.sum(dt.astype(jnp.float32) * o_ref[:HEAD_DIM], 0, keepdims=True) * inv
    over_lanes = (((1,), (1,)), ((), ()))
    for t in range(key_tiles):
        rows = pl.ds(start + t * TILE, TILE)
        e = e_ref[t * TILE:(t + 1) * TILE]
        dp = jnp.dot(vband[rows], dt, preferred_element_type=jnp.float32)
        ds = (e.astype(jnp.float32) * (dp - delta)).astype(jnp.bfloat16)
        ds_all[t * TILE:(t + 1) * TILE] = ds
        dv_acc[rows] += lax.dot_general(e, dt, over_lanes, preferred_element_type=jnp.float32)
        dk_acc[rows] += lax.dot_general(ds, qt, over_lanes, preferred_element_type=jnp.float32)
    dqt = jnp.dot(ktband[:, pl.ds(start, key_tiles * TILE)], ds_all[...],
                  preferred_element_type=jnp.float32) * scale_ref[0]
    for h in range(group):
        dq_ref[:, h * HEAD_DIM:(h + 1) * HEAD_DIM] = dqt[:, h * TILE:(h + 1) * TILE].T.astype(dq_ref.dtype)

    @pl.when(sub == pl.num_programs(1) - 1)
    def _():
        far_rows = dk_far.shape[0]
        dk_far[...] = dk_acc[:far_rows].astype(dk_far.dtype)
        dv_far[...] = dv_acc[:far_rows].astype(dv_far.dtype)
        dk_own[...] = dk_acc[far_rows:]
        dv_own[...] = dv_acc[far_rows:]


def shards(query_rows, key_rows, value_rows, cotangent, slopes, lengths, loss_mask, distances):
    own_q = query_rows[0]
    own_k = key_rows[0]
    own_v = value_rows[0]
    tok_rows, features = own_q.shape
    kv_features = own_k.shape[1]
    head_count = features // HEAD_DIM
    kv_count = kv_features // HEAD_DIM
    group = head_count // kv_count
    reach = (WINDOW - 2) // tok_rows + 1
    band_len = (reach + 1) * tok_rows
    subs = tok_rows // TILE
    key_tiles = WINDOW // TILE + 1
    keys = key_tiles * TILE
    lanes = group * TILE
    n_seq = lax.axis_size("seq")
    n_roll = lax.axis_size("roll")
    seq_len = tok_rows * n_seq
    seq_pos = lax.axis_index("seq")
    roll_pos = lax.axis_index("roll")

    kv_pair = jnp.concatenate([own_k, own_v], 1)
    bands = [passed_along(kv_pair, "seq", offset) for offset in range(reach, 0, -1)] + [kv_pair]
    flipped = flip_blocks(cotangent[0], tok_rows)
    arrived = lax.all_to_all(flipped, "seq", split_axis=0, concat_axis=0, tiled=True)
    dout_t = arrived.reshape(features, tok_rows)
    q_t = flip_blocks(own_q, tok_rows)[0]

    positions = seq_pos * tok_rows + jnp.arange(tok_rows, dtype=jnp.int32)
    valid = ((positions < lengths[0]) & (loss_mask[0] == 1)).astype(jnp.float32)
    mine = jnp.arange(n_roll) == roll_pos
    my_distance = distances[0].astype(jnp.float32)
    sums = lax.psum(
        jnp.stack([jnp.where(mine, jnp.sum(valid), 0.0), jnp.where(mine & (seq_pos == 0), my_distance, 0.0)]),
        ("roll", "seq"))
    count_all = jnp.sum(jnp.where(mine, sums[0], 0.0))
    advantage = (jnp.sum(sums[1]) / n_roll - my_distance) / 64.0
    weight = advantage * seq_len / (1.0 + count_all)

    invalid = jnp.maximum(reach - seq_pos, 0) * subs
    smem = pl.BlockSpec(memory_space=pltpu.SMEM)
    k_specs = [pl.BlockSpec((tok_rows, HEAD_DIM), lambda g, c: (0, g))] * (reach + 1)
    v_specs = [pl.BlockSpec((tok_rows, HEAD_DIM), lambda g, c: (0, kv_count + g))] * (reach + 1)
    t_spec = pl.BlockSpec((group * HEAD_DIM, TILE), lambda g, c: (g, c))
    o_rows = HEAD_DIM + 16
    e_spec = pl.BlockSpec((None, None, keys, lanes), lambda g, c: (g, c, 0, 0))
    o_spec = pl.BlockSpec((None, None, o_rows, lanes), lambda g, c: (g, c, 0, 0))
    params = pltpu.CompilerParams(vmem_limit_bytes=48 << 20)
    pairs = kv_count * group * tok_rows * keys
    e_all, o_all = pl.pallas_call(
        functools.partial(prob_kernel, group, key_tiles),
        grid=(kv_count, subs),
        in_specs=[smem, smem, t_spec, k_specs, v_specs],
        out_specs=(e_spec, o_spec),
        out_shape=(jax.ShapeDtypeStruct((kv_count, subs, keys, lanes), jnp.bfloat16),
                   jax.ShapeDtypeStruct((kv_count, subs, o_rows, lanes), jnp.float32)),
        scratch_shapes=[
            pltpu.VMEM((band_len, HEAD_DIM), jnp.bfloat16),
            pltpu.VMEM((o_rows, band_len), jnp.bfloat16),
            pltpu.VMEM((TILE, lanes), jnp.float32),
            pltpu.VMEM((keys, lanes), jnp.float32),
        ],
        compiler_params=params,
        cost_estimate=pl.CostEstimate(flops=4 * pairs * HEAD_DIM, transcendentals=pairs, bytes_accessed=2 * pairs),
        name="probs",
    )(invalid[None].astype(jnp.int32), slopes, q_t, bands, bands)

    root = 1.0 / math.sqrt(HEAD_DIM)
    far_rows = reach * tok_rows
    far = jax.ShapeDtypeStruct((far_rows, kv_features), jnp.bfloat16)
    own = jax.ShapeDtypeStruct((tok_rows, kv_features), jnp.float32)
    far_spec = pl.BlockSpec((far_rows, HEAD_DIM), lambda g, c: (0, g))
    own_spec = pl.BlockSpec((tok_rows, HEAD_DIM), lambda g, c: (0, g))
    grad_q, far_k, far_v, total_k, total_v = pl.pallas_call(
        functools.partial(grad_kernel, group, key_tiles),
        grid=(kv_count, subs),
        in_specs=[smem, pl.BlockSpec((1, TILE), lambda g, c: (0, c)), t_spec, t_spec, k_specs, v_specs,
                  e_spec, o_spec],
        out_specs=(pl.BlockSpec((TILE, lanes), lambda g, c: (c, g)), far_spec, far_spec, own_spec, own_spec),
        out_shape=(jax.ShapeDtypeStruct((tok_rows, features), jnp.bfloat16), far, far, own, own),
        scratch_shapes=[
            pltpu.VMEM((8, TILE), jnp.bfloat16),
            pltpu.VMEM((HEAD_DIM, band_len), jnp.bfloat16),
            pltpu.VMEM((band_len, HEAD_DIM), jnp.bfloat16),
            pltpu.VMEM((band_len, HEAD_DIM), jnp.float32),
            pltpu.VMEM((band_len, HEAD_DIM), jnp.float32),
            pltpu.VMEM((keys, lanes), jnp.bfloat16),
        ],
        compiler_params=params,
        cost_estimate=pl.CostEstimate(flops=8 * pairs * HEAD_DIM, transcendentals=0, bytes_accessed=2 * pairs),
        name="grads",
    )((weight * root)[None], valid[None], dout_t, q_t, bands, bands, e_all, o_all)

    for offset in range(1, reach + 1):
        rows = slice((reach - offset) * tok_rows, (reach - offset + 1) * tok_rows)
        incoming = passed_along(jnp.concatenate([far_k[rows], far_v[rows]], 1), "seq", -offset).astype(jnp.float32)
        total_k = total_k + incoming[:, :kv_features]
        total_v = total_v + incoming[:, kv_features:]
    total_k = total_k * (weight * root)
    total_v = total_v * weight
    return (grad_q[None], total_k.astype(jnp.bfloat16)[None], total_v.astype(jnp.bfloat16)[None])


def solution(mesh):
    placed = (
        P("roll", "seq", None),
        P("roll", "seq", None),
        P("roll", "seq", None),
        P("roll", None, "seq"),
        P(),
        P("roll"),
        P("roll", "seq"),
        P("roll"),
    )
    return jax.shard_map(
        shards,
        mesh=mesh,
        in_specs=placed,
        out_specs=(P("roll", "seq", None), P("roll", "seq", None), P("roll", "seq", None)),
        check_vma=False,
    )
```

```python
import functools
import math

import jax
import jax.numpy as jnp
from jax import lax
from jax.experimental import pallas as pl
from jax.experimental.pallas import tpu as pltpu
from jax.sharding import PartitionSpec as P

HEAD_DIM = 128
WINDOW = 1024
TILE = 128
FAR = -1e30
LOG2E = math.log2(math.e)
VMEM_LIMIT = 60 << 20
NOTE_ROWS = 16
COVER = 1
COUNT_BASE = 128.0


def passed_along(value, axis, steps):
    count = lax.axis_size(axis)
    leading, last = (max(0, -steps), min(count, count - steps))
    return lax.ppermute(value, axis, [(source, source + steps) for source in range(leading, last)])


def head_of(place, half, near):
    return place // half if near else 1 - place // half


def by_head(value):
    return jnp.concatenate([value[:, n:n + HEAD_DIM] for n in range(0, value.shape[1], HEAD_DIM)], 0)


def flipped_heads(value):
    wide = value.astype(jnp.float32)
    if value.shape[1] == HEAD_DIM:
        return jnp.concatenate([wide[n:n + TILE].T for n in range(0, value.shape[0], TILE)], 1).astype(jnp.bfloat16)
    return jnp.concatenate([wide[:, n:n + TILE].T for n in range(0, value.shape[1], TILE)], 0).astype(jnp.bfloat16)


def gathered(refs, place):
    return [jnp.where(place % 2 == 0, refs[0][...], refs[1][...])] + [ref[...] for ref in refs[2:]]


def split_kernel(half, seq_len, place_ref, length_ref, distance_refs, x_ref, mask_ref, keep_ref, factor_ref, *out_refs):
    place = place_ref[0]
    width, rows = x_ref.shape[0], out_refs[0].shape[1]
    near = place // half
    at = place * rows + lax.broadcasted_iota(jnp.int32, mask_ref.shape, 1)
    keep = jnp.where((at < length_ref[0]) & (mask_ref[...] == 1), 1.0, 0.0)
    keep_ref[...] = keep
    distance = [ref[0].astype(jnp.float32) for ref in distance_refs]
    advantage = (sum(distance) * (1.0 / len(distance)) - distance[0]) * (1.0 / 64.0)
    factor_ref[...] = jnp.full(factor_ref.shape, advantage * seq_len, jnp.float32)
    count = jnp.sum(keep, 1, keepdims=True)
    high = jnp.floor(count * (1.0 / COUNT_BASE))
    notes = jnp.where(lax.broadcasted_iota(jnp.int32, (NOTE_ROWS, rows), 0) == 0, high, count - COUNT_BASE * high)
    for n, out_ref in enumerate(out_refs):
        to = (near if n < half else 1 - near) * half + (place % half + n) % half
        out_ref[:width] = x_ref[:, pl.ds(pl.multiple_of(to * rows, TILE), rows)]
        out_ref[width:] = notes.astype(out_ref.dtype)


def counted(part_refs):
    total = 0.0
    for part_ref in part_refs:
        notes = part_ref[part_ref.shape[0] - NOTE_ROWS:, :128].astype(jnp.float32)
        total = total + COUNT_BASE * notes[:1] + notes[1:2]
    return total


def load_keys(place, k_refs, v_refs, kband, vtband):
    for n, (k, v) in enumerate(zip(gathered(k_refs, place), gathered(v_refs, place))):
        rows = slice(n * k.shape[0], (n + 1) * k.shape[0])
        kband[rows] = k
        vtband[:HEAD_DIM, rows] = v.astype(jnp.float32).T.astype(vtband.dtype)
    vtband[HEAD_DIM:] = jnp.ones(vtband[HEAD_DIM:].shape, vtband.dtype)


def load_grads(place, half, k_refs, v_refs, part_refs, ktband, vband, dk_acc, dv_acc, dt_all):
    for n, (k, v) in enumerate(zip(gathered(k_refs, place), gathered(v_refs, place))):
        rows = slice(n * k.shape[0], (n + 1) * k.shape[0])
        ktband[:, rows] = k.astype(jnp.float32).T.astype(ktband.dtype)
        vband[rows] = v
    dk_acc[...] = jnp.zeros(dk_acc.shape, dk_acc.dtype)
    dv_acc[...] = jnp.zeros(dv_acc.shape, dv_acc.dtype)
    for n, part_ref in enumerate(part_refs):
        width = part_ref.shape[0] - NOTE_ROWS
        source = (place % half + half - n) % half
        part = part_ref[:width].astype(jnp.float32)
        for c in range(dt_all.shape[0]):
            dt_all[c, pl.ds(pl.multiple_of(source * width, 8), width)] = part[:, c * TILE:(c + 1) * TILE]


def slope_lanes(slope_ref, first, group):
    return jnp.concatenate([jnp.full((1, TILE), slope_ref[first + h] * LOG2E, jnp.float32) for h in range(group)], 1)


def load_bias(slope_row, bias):
    bias[...] = lax.broadcasted_iota(jnp.int32, bias.shape, 0).astype(jnp.float32) * slope_row


def soften(sub, place, reach, subs, slope_row, q, kband, vtband, bias, scores, e_ref):
    keys, lanes = scores.shape
    key_tiles = keys // TILE
    scale = LOG2E / math.sqrt(HEAD_DIM)
    qt = flipped_heads(q)
    below = (lax.broadcasted_iota(jnp.int32, (TILE, lanes), 0)
             > lax.broadcasted_iota(jnp.int32, (TILE, lanes), 1) % TILE)
    start = pl.multiple_of(sub * TILE, TILE)
    invalid = jnp.maximum(reach - place, 0) * subs
    peak = None
    shifts = []
    for t in range(key_tiles):
        k_tile = kband[pl.ds(start + t * TILE, TILE)]
        s = jnp.dot(k_tile, qt, preferred_element_type=jnp.float32) * scale + bias[...]
        if t == 0:
            s = jnp.where(below, s, FAR)
        elif t == key_tiles - 1:
            s = jnp.where(below, FAR, s)
        scores[t * TILE:(t + 1) * TILE] = s
        shift = slope_row * (t * TILE) + jnp.where(sub + t < invalid, FAR, 0.0)
        shifts.append(shift)
        top = jnp.max(s.reshape(TILE // 8, 8, lanes), 0) + shift
        peak = top if peak is None else jnp.maximum(peak, top)
    peak = jnp.max(peak, 0, keepdims=True)
    for t in range(key_tiles):
        e = jnp.exp2(scores[t * TILE:(t + 1) * TILE] - (peak - shifts[t]))
        e_ref[t * TILE:(t + 1) * TILE] = e.astype(e_ref.dtype)
    return jnp.dot(vtband[:, pl.ds(start, keys)], e_ref[...], preferred_element_type=jnp.float32)


def differentiate(sub, keep, q, o, e_ref, ktband, vband, dk_acc, dv_acc, ds_all, dt_all):
    keys, lanes = ds_all.shape
    start = pl.multiple_of(sub * TILE, TILE)
    keep = jnp.concatenate([keep] * (lanes // TILE), 1)
    inv = 1.0 / o[HEAD_DIM:HEAD_DIM + 1]
    dt = jnp.concatenate([dt_all[sub, n:n + HEAD_DIM] for n in range(0, lanes, TILE)], 1)
    dt = (dt * (keep * inv)).astype(jnp.bfloat16)
    d = flipped_heads(dt)
    delta = jnp.sum(dt.astype(jnp.float32) * o[:HEAD_DIM], 0, keepdims=True) * inv
    for t in range(keys // TILE):
        rows = pl.ds(start + t * TILE, TILE)
        e = e_ref[t * TILE:(t + 1) * TILE]
        dp = jnp.dot(vband[rows], dt, preferred_element_type=jnp.float32)
        ds = (e.astype(jnp.float32) * (dp - delta)).astype(jnp.bfloat16)
        ds_all[t * TILE:(t + 1) * TILE] = ds
        dv_acc[rows] += jnp.dot(e, d, preferred_element_type=jnp.float32)
        dk_acc[rows] += jnp.dot(ds, q, preferred_element_type=jnp.float32)
    return jnp.dot(ktband[:, pl.ds(start, keys)], ds_all[...], preferred_element_type=jnp.float32)


def store_sums(out_refs, dk_acc, dv_acc):
    for n, out_ref in enumerate(out_refs):
        rows = slice(n * out_ref.shape[0], (n + 1) * out_ref.shape[0])
        out_ref[:, :HEAD_DIM] = dk_acc[rows].astype(out_ref.dtype)
        out_ref[:, HEAD_DIM:] = dv_acc[rows].astype(out_ref.dtype)


def near_kernel(half, reach, place_ref, slope_ref, keep_ref, q_ref, k_refs, v_refs, part_refs,
                dqt_ref, far_two, far_one, own_ref, count_ref,
                kband, vtband, bias, scores, e_all, ktband, vband, dk_acc, dv_acc, ds_all, dt_all):
    place = place_ref[0]
    sub, subs = pl.program_id(0), pl.num_programs(0)
    group = scores.shape[1] // TILE
    slope_row = slope_lanes(slope_ref, head_of(place, half, True) * group, group)

    @pl.when(sub == 0)
    def _():
        load_keys(place, k_refs, v_refs, kband, vtband)
        load_bias(slope_row, bias)
        load_grads(place, half, k_refs, v_refs, part_refs, ktband, vband, dk_acc, dv_acc, dt_all)

    q = by_head(q_ref[...])
    o = soften(sub, place, reach, subs, slope_row, q, kband, vtband, bias, scores, e_all)
    dqt_ref[...] = differentiate(sub, keep_ref[...], q, o, e_all, ktband, vband, dk_acc, dv_acc, ds_all, dt_all)

    @pl.when(sub == subs - 1)
    def _():
        count_ref[...] = jnp.broadcast_to(counted(part_refs), count_ref.shape)
        store_sums((far_two, far_one, own_ref), dk_acc, dv_acc)


def prob_kernel(half, reach, place_ref, slope_ref, q_ref, k_refs, v_refs, e_ref, o_ref, kband, vtband, bias, scores):
    place = place_ref[0]
    sub, subs = pl.program_id(0), pl.num_programs(0)
    group = scores.shape[1] // TILE
    slope_row = slope_lanes(slope_ref, head_of(place, half, False) * group, group)

    @pl.when(sub == 0)
    def _():
        load_keys(place, k_refs, v_refs, kband, vtband)
        load_bias(slope_row, bias)

    o_ref[...] = soften(sub, place, reach, subs, slope_row, by_head(q_ref[...]), kband, vtband, bias, scores, e_ref)


def grad_kernel(half, place_ref, factor_ref, keep_ref, q_ref, k_refs, v_refs, e_ref, o_ref, part_refs, near_dqt, count_ref,
                dq_ref, far_two, far_one, own_ref, weight_ref, ktband, vband, dk_acc, dv_acc, ds_all, dt_all):
    place = place_ref[0]
    sub = pl.program_id(0)
    lanes = ds_all.shape[1]

    @pl.when(sub == 0)
    def _():
        load_grads(place, half, k_refs, v_refs, part_refs, ktband, vband, dk_acc, dv_acc, dt_all)

    dqt = differentiate(sub, keep_ref[...], by_head(q_ref[...]), o_ref, e_ref, ktband, vband, dk_acc, dv_acc, ds_all,
                        dt_all)
    weight = factor_ref[:1] / (1.0 + count_ref[:1] + counted(part_refs))
    weight_ref[...] = jnp.broadcast_to(weight, weight_ref.shape)
    near = place // half
    for first, value in ((near * lanes, near_dqt[...]), ((1 - near) * lanes, dqt)):
        for n in range(0, lanes, TILE):
            cols = pl.ds(pl.multiple_of(first + n, TILE), TILE)
            dq_ref[:, cols] = (value[:, n:n + TILE].T * (weight * (1.0 / math.sqrt(HEAD_DIM)))).astype(dq_ref.dtype)

    @pl.when(sub == pl.num_programs(0) - 1)
    def _():
        store_sums((far_two, far_one, own_ref), dk_acc, dv_acc)


def returned_sums(place, half, total, back_refs, near):
    for n, back_ref in enumerate(back_refs):
        same = ((place + 1 + n) // half == place // half) == near
        back = back_ref[...].astype(jnp.float32)
        total = [total[0] + jnp.where(same, back, 0.0), total[1] + jnp.where(same, 0.0, back)]
    return total


def early_kernel(half, place_ref, own_near, own_other, back_refs, near_total, other_total):
    near_total[...], other_total[...] = returned_sums(
        place_ref[0], half, [own_near[...], own_other[...]], back_refs, True)


def final_kernel(half, place_ref, weight_ref, near_total, other_total, back_refs, dk_ref, dv_ref):
    place = place_ref[0]
    total = returned_sums(place, half, [near_total[...], other_total[...]], back_refs, False)
    high = place // half == 1
    total = [jnp.where(high, total[1], total[0]), jnp.where(high, total[0], total[1])]
    weight = weight_ref[:1, :HEAD_DIM]
    for n, value in enumerate(total):
        cols = slice(n * HEAD_DIM, (n + 1) * HEAD_DIM)
        dk_ref[:, cols] = (value[:, :HEAD_DIM] * (weight * (1.0 / math.sqrt(HEAD_DIM)))).astype(dk_ref.dtype)
        dv_ref[:, cols] = (value[:, HEAD_DIM:] * weight).astype(dv_ref.dtype)


def shards(query_rows, key_rows, value_rows, cotangent, slopes, lengths, loss_mask, distances):
    own_q = query_rows[0]
    own_k = key_rows[0]
    own_v = value_rows[0]
    tok_rows, features = own_q.shape
    kv_features = own_k.shape[1]
    head_count = features // HEAD_DIM
    kv_count = kv_features // HEAD_DIM
    group = head_count // kv_count
    reach = (WINDOW - 2) // tok_rows + 1
    band_len = (reach + 1) * tok_rows
    subs = tok_rows // TILE
    keys = WINDOW + TILE
    lanes = group * TILE
    o_rows = HEAD_DIM + 16
    n_seq = lax.axis_size("seq")
    n_roll = lax.axis_size("roll")
    seq_len = tok_rows * n_seq
    seq_pos = lax.axis_index("seq")
    half = n_seq // kv_count
    width = features // n_seq
    assert kv_count == 2 and width * half == lanes and reach == 2
    place = seq_pos[None].astype(jnp.int32)

    kv_pair = jnp.concatenate([own_k, own_v], 1)
    back_one = passed_along(kv_pair, "seq", 1)
    back_two_even = lax.ppermute(kv_pair, "seq", [(s, s + 2) for s in range(0, n_seq - 2, 2)])

    smem = pl.BlockSpec(memory_space=pltpu.SMEM)
    vmem = pl.BlockSpec(memory_space=pltpu.VMEM)
    params = pltpu.CompilerParams(vmem_limit_bytes=VMEM_LIMIT)
    apart = [distances]
    for shift in range(1, n_roll):
        apart.append(lax.ppermute(distances, "roll", [(n, (n + shift) % n_roll) for n in range(n_roll)]))
    piece = jax.ShapeDtypeStruct((width + NOTE_ROWS, tok_rows), jnp.bfloat16)
    keep, factor, *pieces = pl.pallas_call(
        functools.partial(split_kernel, half, seq_len),
        in_specs=[smem, smem, [smem] * n_roll, vmem, vmem],
        out_specs=[vmem] * (n_seq + 2),
        out_shape=[jax.ShapeDtypeStruct((1, tok_rows), jnp.float32), jax.ShapeDtypeStruct((8, 128), jnp.float32)]
        + [piece] * n_seq,
        compiler_params=params,
        name="split_cotangent",
    )(place, lengths, apart, cotangent[0].T, loss_mask)
    pieces, back_one, back_two_even = lax.optimization_barrier((pieces, back_one, back_two_even))
    parts = {0: pieces[0]}
    for n in list(range(half, n_seq)) + list(range(1, half)):
        pairs = []
        for source in range(n_seq):
            side = source // half if n < half else 1 - source // half
            pairs.append((source, side * half + (source % half + n) % half))
        parts[n] = lax.ppermute(pieces[n], "seq", pairs)
    parts = [parts[n] for n in range(n_seq)]
    back_two_odd = lax.ppermute(back_one, "seq", [(s, s + 1) for s in range(2, n_seq, 2)])
    bands = [back_two_even, back_two_odd, back_one, kv_pair]

    pair_count = group * tok_rows * keys
    bf16, f32 = jnp.bfloat16, jnp.float32

    def head_specs(near, offset):
        spec = pl.BlockSpec((tok_rows, HEAD_DIM), lambda c, at: (0, offset + head_of(at[0], half, near)))
        return [spec] * len(bands)

    def q_spec(near):
        return pl.BlockSpec((TILE, lanes), lambda c, at: (c, head_of(at[0], half, near)))

    keep_spec = pl.BlockSpec((1, TILE), lambda c, at: (0, c))
    e_spec = pl.BlockSpec((None, keys, lanes), lambda c, at: (c, 0, 0))
    o_spec = pl.BlockSpec((None, o_rows, lanes), lambda c, at: (c, 0, 0))
    prob_scratch = [
        pltpu.VMEM((band_len, HEAD_DIM), bf16),
        pltpu.VMEM((o_rows, band_len), bf16),
        pltpu.VMEM((TILE, lanes), f32),
        pltpu.VMEM((keys, lanes), f32),
    ]
    grad_scratch = [
        pltpu.VMEM((HEAD_DIM, band_len), bf16),
        pltpu.VMEM((band_len, HEAD_DIM), bf16),
        pltpu.VMEM((band_len, HEAD_DIM), f32),
        pltpu.VMEM((band_len, HEAD_DIM), f32),
        pltpu.VMEM((keys, lanes), bf16),
        pltpu.VMEM((subs, lanes, TILE), f32),
    ]
    note = jax.ShapeDtypeStruct((8, 128), f32)
    dqt_spec = pl.BlockSpec((None, HEAD_DIM, lanes), lambda c, at: (c, 0, 0))
    grad_shapes = (
        jax.ShapeDtypeStruct((tok_rows, 2 * HEAD_DIM), bf16),
        jax.ShapeDtypeStruct((tok_rows, 2 * HEAD_DIM), bf16),
        jax.ShapeDtypeStruct((tok_rows, 2 * HEAD_DIM), f32),
    )

    def returned(sums):
        return [passed_along(sums[reach - offset], "seq", -offset) for offset in range(1, reach + 1)]

    e_all, o_all = pl.pallas_call(
        functools.partial(prob_kernel, half, reach),
        grid_spec=pltpu.PrefetchScalarGridSpec(
            num_scalar_prefetch=1,
            grid=(subs,),
            in_specs=[smem, q_spec(False), head_specs(False, 0), head_specs(False, kv_count)],
            out_specs=(e_spec, o_spec),
            scratch_shapes=prob_scratch,
        ),
        out_shape=(jax.ShapeDtypeStruct((subs, keys, lanes), bf16), jax.ShapeDtypeStruct((subs, o_rows, lanes), f32)),
        compiler_params=params,
        cost_estimate=pl.CostEstimate(flops=4 * pair_count * HEAD_DIM // COVER, transcendentals=0, bytes_accessed=1 << 16),
        name="other_probs",
    )(place, slopes, own_q, bands, bands)
    late_slopes, o_all = lax.optimization_barrier((slopes, o_all))
    near_dqt, *near_sums, near_count = pl.pallas_call(
        functools.partial(near_kernel, half, reach),
        grid_spec=pltpu.PrefetchScalarGridSpec(
            num_scalar_prefetch=1,
            grid=(subs,),
            in_specs=[smem, keep_spec, q_spec(True), head_specs(True, 0), head_specs(True, kv_count), [vmem] * half],
            out_specs=(dqt_spec, vmem, vmem, vmem, vmem),
            scratch_shapes=prob_scratch + [pltpu.VMEM((keys, lanes), bf16)] + grad_scratch,
        ),
        out_shape=(jax.ShapeDtypeStruct((subs, HEAD_DIM, lanes), f32),) + grad_shapes + (note,),
        compiler_params=params,
        cost_estimate=pl.CostEstimate(flops=12 * pair_count * HEAD_DIM // COVER, transcendentals=0, bytes_accessed=1 << 16),
        name="near_head",
    )(place, late_slopes, keep, own_q, bands, bands, parts[:half])
    near_back = returned(near_sums)
    dq, *other_sums, weight = pl.pallas_call(
        functools.partial(grad_kernel, half),
        grid_spec=pltpu.PrefetchScalarGridSpec(
            num_scalar_prefetch=1,
            grid=(subs,),
            in_specs=[vmem, keep_spec, q_spec(False), head_specs(False, 0), head_specs(False, kv_count), e_spec, o_spec,
                      [vmem] * half, dqt_spec, vmem],
            out_specs=(pl.BlockSpec((TILE, features), lambda c, at: (c, 0)), vmem, vmem, vmem, vmem),
            scratch_shapes=grad_scratch,
        ),
        out_shape=(jax.ShapeDtypeStruct((tok_rows, features), bf16),) + grad_shapes + (note,),
        compiler_params=params,
        cost_estimate=pl.CostEstimate(flops=8 * pair_count * HEAD_DIM // COVER, transcendentals=0, bytes_accessed=1 << 16),
        name="other_grads",
    )(place, factor, keep, own_q, bands, bands, e_all, o_all, parts[half:], near_dqt, near_count)
    other_back = returned(other_sums)

    sums = jax.ShapeDtypeStruct((tok_rows, 2 * HEAD_DIM), f32)
    totals = pl.pallas_call(
        functools.partial(early_kernel, half),
        in_specs=[smem, vmem, vmem, [vmem] * reach],
        out_specs=(vmem, vmem),
        out_shape=(sums, sums),
        name="sum_near",
    )(place, near_sums[-1], other_sums[-1], near_back)
    out = jax.ShapeDtypeStruct((tok_rows, kv_features), bf16)
    grad_k, grad_v = pl.pallas_call(
        functools.partial(final_kernel, half),
        in_specs=[smem, vmem, vmem, vmem, [vmem] * reach],
        out_specs=(vmem, vmem),
        out_shape=(out, out),
        name="sum_other",
    )(place, weight, *totals, other_back)
    return (dq[None], grad_k[None], grad_v[None])


def solution(mesh):
    placed = (
        P("roll", "seq", None),
        P("roll", "seq", None),
        P("roll", "seq", None),
        P("roll", None, "seq"),
        P(),
        P("roll"),
        P("roll", "seq"),
        P("roll"),
    )
    return jax.shard_map(
        shards,
        mesh=mesh,
        in_specs=placed,
        out_specs=(P("roll", "seq", None), P("roll", "seq", None), P("roll", "seq", None)),
        check_vma=False,
    )
```

```python
import functools
import math

import jax
import jax.numpy as jnp
from jax import lax
from jax.experimental import pallas as pl
from jax.experimental.pallas import tpu as pltpu
from jax.sharding import PartitionSpec as P

HEAD_DIM = 128
WINDOW = 1024
TILE = 128
FAR = -1e30
LOG2E = math.log2(math.e)
VMEM_LIMIT = 24 << 20
NOTE_ROWS = 16
COVER = 1
NEAR_COVER = 1
COUNT_BASE = 128.0


def passed_along(value, axis, steps):
    count = lax.axis_size(axis)
    leading, last = (max(0, -steps), min(count, count - steps))
    return lax.ppermute(value, axis, [(source, source + steps) for source in range(leading, last)])


def head_of(place, half, near):
    return place // half if near else 1 - place // half


def by_head(value):
    return jnp.concatenate([value[:, n:n + HEAD_DIM] for n in range(0, value.shape[1], HEAD_DIM)], 0)


def flipped_heads(value):
    wide = value.astype(jnp.float32)
    if value.shape[1] == HEAD_DIM:
        return jnp.concatenate([wide[n:n + TILE].T for n in range(0, value.shape[0], TILE)], 1).astype(jnp.bfloat16)
    return jnp.concatenate([wide[:, n:n + TILE].T for n in range(0, value.shape[1], TILE)], 0).astype(jnp.bfloat16)


def gathered(refs, place):
    return [jnp.where(place % 2 == 0, refs[0][...], refs[1][...])] + [ref[...] for ref in refs[2:]]


def split_kernel(half, place_ref, length_ref, x_ref, mask_ref, keep_ref, *out_refs):
    place = place_ref[0]
    width, rows = x_ref.shape[0], out_refs[0].shape[1]
    near = place // half
    at = place * rows + lax.broadcasted_iota(jnp.int32, mask_ref.shape, 1)
    keep = jnp.where((at < length_ref[0]) & (mask_ref[...] == 1), 1.0, 0.0)
    keep_ref[...] = keep
    count = jnp.sum(keep, 1, keepdims=True)
    high = jnp.floor(count * (1.0 / COUNT_BASE))
    notes = jnp.where(lax.broadcasted_iota(jnp.int32, (NOTE_ROWS, rows), 0) == 0, high, count - COUNT_BASE * high)
    for n, out_ref in enumerate(out_refs):
        to = (near if n < half else 1 - near) * half + (place % half + n) % half
        out_ref[:width] = x_ref[:, pl.ds(pl.multiple_of(to * rows, TILE), rows)]
        out_ref[width:] = notes.astype(out_ref.dtype)


def counted(part_refs):
    total = 0.0
    for part_ref in part_refs:
        notes = part_ref[part_ref.shape[0] - NOTE_ROWS:, :128].astype(jnp.float32)
        total = total + COUNT_BASE * notes[:1] + notes[1:2]
    return total


def load_keys(place, k_refs, v_refs, kband, vtband):
    for n, (k, v) in enumerate(zip(gathered(k_refs, place), gathered(v_refs, place))):
        rows = slice(n * k.shape[0], (n + 1) * k.shape[0])
        kband[rows] = k
        vtband[:HEAD_DIM, rows] = v.astype(jnp.float32).T.astype(vtband.dtype)
    vtband[HEAD_DIM:] = jnp.ones(vtband[HEAD_DIM:].shape, vtband.dtype)


def load_grads(place, half, k_refs, v_refs, part_refs, ktband, vband, dk_acc, dv_acc, dt_all):
    for n, (k, v) in enumerate(zip(gathered(k_refs, place), gathered(v_refs, place))):
        rows = slice(n * k.shape[0], (n + 1) * k.shape[0])
        ktband[:, rows] = k.astype(jnp.float32).T.astype(ktband.dtype)
        vband[rows] = v
    dk_acc[...] = jnp.zeros(dk_acc.shape, dk_acc.dtype)
    dv_acc[...] = jnp.zeros(dv_acc.shape, dv_acc.dtype)
    for n, part_ref in enumerate(part_refs):
        width = part_ref.shape[0] - NOTE_ROWS
        source = (place % half + half - n) % half
        part = part_ref[:width].astype(jnp.float32)
        for c in range(dt_all.shape[0]):
            dt_all[c, pl.ds(pl.multiple_of(source * width, 8), width)] = part[:, c * TILE:(c + 1) * TILE]


def slope_lanes(slope_ref, first, group):
    return jnp.concatenate([jnp.full((1, TILE), slope_ref[first + h] * LOG2E, jnp.float32) for h in range(group)], 1)


def load_bias(slope_row, bias):
    bias[...] = lax.broadcasted_iota(jnp.int32, bias.shape, 0).astype(jnp.float32) * slope_row


def soften(sub, place, reach, subs, slope_row, q, kband, vtband, bias, scores, e_ref):
    keys, lanes = scores.shape
    key_tiles = keys // TILE
    scale = LOG2E / math.sqrt(HEAD_DIM)
    qt = flipped_heads(q)
    below = (lax.broadcasted_iota(jnp.int32, (TILE, lanes), 0)
             > lax.broadcasted_iota(jnp.int32, (TILE, lanes), 1) % TILE)
    start = pl.multiple_of(sub * TILE, TILE)
    invalid = jnp.maximum(reach - place, 0) * subs
    peak = None
    shifts = []
    for t in range(key_tiles):
        k_tile = kband[pl.ds(start + t * TILE, TILE)]
        s = jnp.dot(k_tile, qt, preferred_element_type=jnp.float32) * scale + bias[...]
        if t == 0:
            s = jnp.where(below, s, FAR)
        elif t == key_tiles - 1:
            s = jnp.where(below, FAR, s)
        scores[t * TILE:(t + 1) * TILE] = s
        shift = slope_row * (t * TILE) + jnp.where(sub + t < invalid, FAR, 0.0)
        shifts.append(shift)
        top = jnp.max(s.reshape(TILE // 8, 8, lanes), 0) + shift
        peak = top if peak is None else jnp.maximum(peak, top)
    peak = jnp.max(peak, 0, keepdims=True)
    for t in range(key_tiles):
        e = jnp.exp2(scores[t * TILE:(t + 1) * TILE] - (peak - shifts[t]))
        e_ref[t * TILE:(t + 1) * TILE] = e.astype(e_ref.dtype)
    return jnp.dot(vtband[:, pl.ds(start, keys)], e_ref[...], preferred_element_type=jnp.float32)


def differentiate(sub, keep, q, o, e_ref, ktband, vband, dk_acc, dv_acc, ds_all, dt_all):
    keys, lanes = ds_all.shape
    start = pl.multiple_of(sub * TILE, TILE)
    keep = jnp.concatenate([keep] * (lanes // TILE), 1)
    inv = 1.0 / o[HEAD_DIM:HEAD_DIM + 1]
    dt = jnp.concatenate([dt_all[sub, n:n + HEAD_DIM] for n in range(0, lanes, TILE)], 1)
    dt = (dt * (keep * inv)).astype(jnp.bfloat16)
    d = flipped_heads(dt)
    delta = jnp.sum(dt.astype(jnp.float32) * o[:HEAD_DIM], 0, keepdims=True) * inv
    for t in range(keys // TILE):
        rows = pl.ds(start + t * TILE, TILE)
        e = e_ref[t * TILE:(t + 1) * TILE]
        dp = jnp.dot(vband[rows], dt, preferred_element_type=jnp.float32)
        ds = (e.astype(jnp.float32) * (dp - delta)).astype(jnp.bfloat16)
        ds_all[t * TILE:(t + 1) * TILE] = ds
        dv_acc[rows] += jnp.dot(e, d, preferred_element_type=jnp.float32)
        dk_acc[rows] += jnp.dot(ds, q, preferred_element_type=jnp.float32)
    return jnp.dot(ktband[:, pl.ds(start, keys)], ds_all[...], preferred_element_type=jnp.float32)


def store_sums(out_refs, dk_acc, dv_acc):
    for n, out_ref in enumerate(out_refs):
        rows = slice(n * out_ref.shape[0], (n + 1) * out_ref.shape[0])
        out_ref[:, :HEAD_DIM] = dk_acc[rows].astype(out_ref.dtype)
        out_ref[:, HEAD_DIM:] = dv_acc[rows].astype(out_ref.dtype)


def near_kernel(half, reach, place_ref, slope_ref, keep_ref, q_ref, k_refs, v_refs, part_refs,
                dqt_ref, far_two, far_one, own_ref, count_ref,
                kband, vtband, bias, scores, e_all, ktband, vband, dk_acc, dv_acc, ds_all, dt_all):
    place = place_ref[0]
    sub, subs = pl.program_id(0), pl.num_programs(0)
    group = scores.shape[1] // TILE
    slope_row = slope_lanes(slope_ref, head_of(place, half, True) * group, group)

    @pl.when(sub == 0)
    def _():
        load_keys(place, k_refs, v_refs, kband, vtband)
        load_bias(slope_row, bias)
        load_grads(place, half, k_refs, v_refs, part_refs, ktband, vband, dk_acc, dv_acc, dt_all)

    q = by_head(q_ref[...])
    o = soften(sub, place, reach, subs, slope_row, q, kband, vtband, bias, scores, e_all)
    dqt_ref[...] = differentiate(sub, keep_ref[...], q, o, e_all, ktband, vband, dk_acc, dv_acc, ds_all, dt_all)

    @pl.when(sub == subs - 1)
    def _():
        count_ref[...] = jnp.broadcast_to(counted(part_refs), count_ref.shape)
        store_sums((far_two, far_one, own_ref), dk_acc, dv_acc)


def prob_kernel(half, reach, place_ref, slope_ref, q_ref, k_refs, v_refs, e_ref, o_ref, kband, vtband, bias, scores):
    place = place_ref[0]
    sub, subs = pl.program_id(0), pl.num_programs(0)
    group = scores.shape[1] // TILE
    slope_row = slope_lanes(slope_ref, head_of(place, half, False) * group, group)

    @pl.when(sub == 0)
    def _():
        load_keys(place, k_refs, v_refs, kband, vtband)
        load_bias(slope_row, bias)

    o_ref[...] = soften(sub, place, reach, subs, slope_row, by_head(q_ref[...]), kband, vtband, bias, scores, e_ref)


def grad_kernel(half, place_ref, factor_ref, keep_ref, q_ref, k_refs, v_refs, e_ref, o_ref, part_refs, near_dqt, count_ref,
                dq_ref, far_two, far_one, own_ref, weight_ref, ktband, vband, dk_acc, dv_acc, ds_all, dt_all):
    place = place_ref[0]
    sub = pl.program_id(0)
    lanes = ds_all.shape[1]

    @pl.when(sub == 0)
    def _():
        load_grads(place, half, k_refs, v_refs, part_refs, ktband, vband, dk_acc, dv_acc, dt_all)

    dqt = differentiate(sub, keep_ref[...], by_head(q_ref[...]), o_ref, e_ref, ktband, vband, dk_acc, dv_acc, ds_all,
                        dt_all)
    weight = factor_ref[:1] / (1.0 + count_ref[:1] + counted(part_refs))
    weight_ref[...] = jnp.broadcast_to(weight, weight_ref.shape)
    near = place // half
    for first, value in ((near * lanes, near_dqt[...]), ((1 - near) * lanes, dqt)):
        for n in range(0, lanes, TILE):
            cols = pl.ds(pl.multiple_of(first + n, TILE), TILE)
            dq_ref[:, cols] = (value[:, n:n + TILE].T * (weight * (1.0 / math.sqrt(HEAD_DIM)))).astype(dq_ref.dtype)

    @pl.when(sub == pl.num_programs(0) - 1)
    def _():
        store_sums((far_two, far_one, own_ref), dk_acc, dv_acc)


def returned_sums(place, half, total, back_refs, near):
    for n, back_ref in enumerate(back_refs):
        same = ((place + 1 + n) // half == place // half) == near
        back = back_ref[...].astype(jnp.float32)
        total = [total[0] + jnp.where(same, back, 0.0), total[1] + jnp.where(same, 0.0, back)]
    return total


def early_kernel(half, place_ref, own_near, own_other, back_refs, near_total, other_total):
    near_total[...], other_total[...] = returned_sums(
        place_ref[0], half, [own_near[...], own_other[...]], back_refs, True)


def final_kernel(half, place_ref, weight_ref, near_total, other_total, back_refs, dk_ref, dv_ref):
    place = place_ref[0]
    total = returned_sums(place, half, [near_total[...], other_total[...]], back_refs, False)
    high = place // half == 1
    total = [jnp.where(high, total[1], total[0]), jnp.where(high, total[0], total[1])]
    weight = weight_ref[:1, :HEAD_DIM]
    for n, value in enumerate(total):
        cols = slice(n * HEAD_DIM, (n + 1) * HEAD_DIM)
        dk_ref[:, cols] = (value[:, :HEAD_DIM] * (weight * (1.0 / math.sqrt(HEAD_DIM)))).astype(dk_ref.dtype)
        dv_ref[:, cols] = (value[:, HEAD_DIM:] * weight).astype(dv_ref.dtype)


def shards(query_rows, key_rows, value_rows, cotangent, slopes, lengths, loss_mask, distances):
    own_q = query_rows[0]
    own_k = key_rows[0]
    own_v = value_rows[0]
    tok_rows, features = own_q.shape
    kv_features = own_k.shape[1]
    head_count = features // HEAD_DIM
    kv_count = kv_features // HEAD_DIM
    group = head_count // kv_count
    reach = (WINDOW - 2) // tok_rows + 1
    band_len = (reach + 1) * tok_rows
    subs = tok_rows // TILE
    keys = WINDOW + TILE
    lanes = group * TILE
    o_rows = HEAD_DIM + 16
    n_seq = lax.axis_size("seq")
    n_roll = lax.axis_size("roll")
    seq_len = tok_rows * n_seq
    seq_pos = lax.axis_index("seq")
    half = n_seq // kv_count
    width = features // n_seq
    assert kv_count == 2 and width * half == lanes and reach == 2
    place = seq_pos[None].astype(jnp.int32)

    kv_pair = jnp.concatenate([own_k, own_v], 1)
    back_one = passed_along(kv_pair, "seq", 1)
    back_two_even = lax.ppermute(kv_pair, "seq", [(s, s + 2) for s in range(0, n_seq - 2, 2)])

    smem = pl.BlockSpec(memory_space=pltpu.SMEM)
    vmem = pl.BlockSpec(memory_space=pltpu.VMEM)
    params = pltpu.CompilerParams(vmem_limit_bytes=VMEM_LIMIT)
    piece = jax.ShapeDtypeStruct((width + NOTE_ROWS, tok_rows), jnp.bfloat16)
    keep, *pieces = pl.pallas_call(
        functools.partial(split_kernel, half),
        in_specs=[smem, smem, vmem, vmem],
        out_specs=[vmem] * (n_seq + 1),
        out_shape=[jax.ShapeDtypeStruct((1, tok_rows), jnp.float32)]
        + [piece] * n_seq,
        compiler_params=params,
        name="split_cotangent",
    )(place, lengths, cotangent[0].T, loss_mask)
    apart = [distances]
    for shift in range(1, n_roll):
        apart.append(lax.ppermute(distances, "roll", [(n, (n + shift) % n_roll) for n in range(n_roll)]))
    pieces, back_one, apart = lax.optimization_barrier((pieces, back_one, apart))
    apart = [distance[0].astype(jnp.float32) for distance in apart]
    factor = jnp.broadcast_to((sum(apart) / n_roll - apart[0]) / 64.0 * seq_len, (8, 128))
    parts = {0: pieces[0]}
    for n in list(range(half, n_seq)) + list(range(1, half)):
        pairs = []
        for source in range(n_seq):
            side = source // half if n < half else 1 - source // half
            pairs.append((source, side * half + (source % half + n) % half))
        parts[n] = lax.ppermute(pieces[n], "seq", pairs)
    parts = [parts[n] for n in range(n_seq)]
    back_two_odd = lax.ppermute(back_one, "seq", [(s, s + 1) for s in range(2, n_seq, 2)])
    bands = [back_two_even, back_two_odd, back_one, kv_pair]

    pair_count = group * tok_rows * keys
    bf16, f32 = jnp.bfloat16, jnp.float32

    def head_specs(near, offset):
        spec = pl.BlockSpec((tok_rows, HEAD_DIM), lambda c, at: (0, offset + head_of(at[0], half, near)))
        return [spec] * len(bands)

    def q_spec(near):
        return pl.BlockSpec((TILE, lanes), lambda c, at: (c, head_of(at[0], half, near)))

    keep_spec = pl.BlockSpec((1, TILE), lambda c, at: (0, c))
    e_spec = pl.BlockSpec((None, keys, lanes), lambda c, at: (c, 0, 0))
    o_spec = pl.BlockSpec((None, o_rows, lanes), lambda c, at: (c, 0, 0))
    prob_scratch = [
        pltpu.VMEM((band_len, HEAD_DIM), bf16),
        pltpu.VMEM((o_rows, band_len), bf16),
        pltpu.VMEM((TILE, lanes), f32),
        pltpu.VMEM((keys, lanes), f32),
    ]
    grad_scratch = [
        pltpu.VMEM((HEAD_DIM, band_len), bf16),
        pltpu.VMEM((band_len, HEAD_DIM), bf16),
        pltpu.VMEM((band_len, HEAD_DIM), f32),
        pltpu.VMEM((band_len, HEAD_DIM), f32),
        pltpu.VMEM((keys, lanes), bf16),
        pltpu.VMEM((subs, lanes, TILE), f32),
    ]
    note = jax.ShapeDtypeStruct((8, 128), f32)
    dqt_spec = pl.BlockSpec((None, HEAD_DIM, lanes), lambda c, at: (c, 0, 0))
    grad_shapes = (
        jax.ShapeDtypeStruct((tok_rows, 2 * HEAD_DIM), bf16),
        jax.ShapeDtypeStruct((tok_rows, 2 * HEAD_DIM), bf16),
        jax.ShapeDtypeStruct((tok_rows, 2 * HEAD_DIM), f32),
    )

    def returned(sums):
        return [passed_along(sums[reach - offset], "seq", -offset) for offset in range(1, reach + 1)]

    e_all, o_all = pl.pallas_call(
        functools.partial(prob_kernel, half, reach),
        grid_spec=pltpu.PrefetchScalarGridSpec(
            num_scalar_prefetch=1,
            grid=(subs,),
            in_specs=[smem, q_spec(False), head_specs(False, 0), head_specs(False, kv_count)],
            out_specs=(e_spec, o_spec),
            scratch_shapes=prob_scratch,
        ),
        out_shape=(jax.ShapeDtypeStruct((subs, keys, lanes), bf16), jax.ShapeDtypeStruct((subs, o_rows, lanes), f32)),
        compiler_params=params,
        cost_estimate=pl.CostEstimate(flops=4 * pair_count * HEAD_DIM // COVER, transcendentals=0, bytes_accessed=1 << 16),
        name="other_probs",
    )(place, slopes, own_q, bands, bands)
    late_slopes, o_all = lax.optimization_barrier((slopes, o_all))
    near_dqt, *near_sums, near_count = pl.pallas_call(
        functools.partial(near_kernel, half, reach),
        grid_spec=pltpu.PrefetchScalarGridSpec(
            num_scalar_prefetch=1,
            grid=(subs,),
            in_specs=[smem, keep_spec, q_spec(True), head_specs(True, 0), head_specs(True, kv_count), [vmem] * half],
            out_specs=(dqt_spec, vmem, vmem, vmem, vmem),
            scratch_shapes=prob_scratch + [pltpu.VMEM((keys, lanes), bf16)] + grad_scratch,
        ),
        out_shape=(jax.ShapeDtypeStruct((subs, HEAD_DIM, lanes), f32),) + grad_shapes + (note,),
        compiler_params=params,
        cost_estimate=pl.CostEstimate(flops=12 * pair_count * HEAD_DIM // NEAR_COVER, transcendentals=0, bytes_accessed=1 << 16),
        name="near_head",
    )(place, late_slopes, keep, own_q, bands, bands, parts[:half])
    near_back = returned(near_sums)
    dq, *other_sums, weight = pl.pallas_call(
        functools.partial(grad_kernel, half),
        grid_spec=pltpu.PrefetchScalarGridSpec(
            num_scalar_prefetch=1,
            grid=(subs,),
            in_specs=[vmem, keep_spec, q_spec(False), head_specs(False, 0), head_specs(False, kv_count), e_spec, o_spec,
                      [vmem] * half, dqt_spec, vmem],
            out_specs=(pl.BlockSpec((TILE, features), lambda c, at: (c, 0)), vmem, vmem, vmem, vmem),
            scratch_shapes=grad_scratch,
        ),
        out_shape=(jax.ShapeDtypeStruct((tok_rows, features), bf16),) + grad_shapes + (note,),
        compiler_params=params,
        cost_estimate=pl.CostEstimate(flops=8 * pair_count * HEAD_DIM // COVER, transcendentals=0, bytes_accessed=1 << 16),
        name="other_grads",
    )(place, factor, keep, own_q, bands, bands, e_all, o_all, parts[half:], near_dqt, near_count)
    other_back = returned(other_sums)

    sums = jax.ShapeDtypeStruct((tok_rows, 2 * HEAD_DIM), f32)
    totals = pl.pallas_call(
        functools.partial(early_kernel, half),
        in_specs=[smem, vmem, vmem, [vmem] * reach],
        out_specs=(vmem, vmem),
        out_shape=(sums, sums),
        compiler_params=pltpu.CompilerParams(vmem_limit_bytes=8 << 20),
        name="sum_near",
    )(place, near_sums[-1], other_sums[-1], near_back)
    out = jax.ShapeDtypeStruct((tok_rows, kv_features), bf16)
    grad_k, grad_v = pl.pallas_call(
        functools.partial(final_kernel, half),
        in_specs=[smem, vmem, vmem, vmem, [vmem] * reach],
        out_specs=(vmem, vmem),
        out_shape=(out, out),
        compiler_params=pltpu.CompilerParams(vmem_limit_bytes=8 << 20),
        name="sum_other",
    )(place, weight, *totals, other_back)
    return (dq[None], grad_k[None], grad_v[None])


def solution(mesh):
    placed = (
        P("roll", "seq", None),
        P("roll", "seq", None),
        P("roll", "seq", None),
        P("roll", None, "seq"),
        P(),
        P("roll"),
        P("roll", "seq"),
        P("roll"),
    )
    return jax.shard_map(
        shards,
        mesh=mesh,
        in_specs=placed,
        out_specs=(P("roll", "seq", None), P("roll", "seq", None), P("roll", "seq", None)),
        check_vma=False,
    )
```

```python
import functools
import math

import jax
import jax.numpy as jnp
from jax import lax
from jax.experimental import pallas as pl
from jax.experimental.pallas import tpu as pltpu
from jax.sharding import PartitionSpec as P

HEAD_DIM = 128
WINDOW = 1024
TILE = 128
FAR = -1e30
LOG2E = math.log2(math.e)
VMEM_LIMIT = 24 << 20
NOTE_ROWS = 8
COVER = 1
NEAR_COVER = 1
COUNT_BASE = 128.0


def passed_along(value, axis, steps):
    count = lax.axis_size(axis)
    leading, last = (max(0, -steps), min(count, count - steps))
    return lax.ppermute(value, axis, [(source, source + steps) for source in range(leading, last)])


def head_of(place, half, near):
    return place // half if near else 1 - place // half


def by_head(value):
    return jnp.concatenate([value[:, n:n + HEAD_DIM] for n in range(0, value.shape[1], HEAD_DIM)], 0)


def flipped_heads(value):
    wide = value.astype(jnp.float32)
    if value.shape[1] == HEAD_DIM:
        return jnp.concatenate([wide[n:n + TILE].T for n in range(0, value.shape[0], TILE)], 1).astype(jnp.bfloat16)
    return jnp.concatenate([wide[:, n:n + TILE].T for n in range(0, value.shape[1], TILE)], 0).astype(jnp.bfloat16)


def gathered(refs, place):
    return [jnp.where(place % 2 == 0, refs[0][...], refs[1][...])] + [ref[...] for ref in refs[2:]]


def split_kernel(half, place_ref, length_ref, x_ref, mask_ref, keep_ref, *out_refs):
    place = place_ref[0]
    width, rows = x_ref.shape[0], out_refs[0].shape[1]
    near = place // half
    at = place * rows + lax.broadcasted_iota(jnp.int32, mask_ref.shape, 1)
    keep = jnp.where((at < length_ref[0]) & (mask_ref[...] == 1), 1.0, 0.0)
    keep_ref[...] = keep
    count = jnp.sum(keep, 1, keepdims=True)
    high = jnp.floor(count * (1.0 / COUNT_BASE))
    notes = jnp.where(lax.broadcasted_iota(jnp.int32, (NOTE_ROWS, rows), 0) == 0, high, count - COUNT_BASE * high)
    for n, out_ref in enumerate(out_refs):
        to = (near if n < half else 1 - near) * half + (place % half + n) % half
        out_ref[:width] = x_ref[:, pl.ds(pl.multiple_of(to * rows, TILE), rows)]
        out_ref[width:] = notes.astype(out_ref.dtype)


def counted(part_refs):
    total = 0.0
    for part_ref in part_refs:
        notes = part_ref[part_ref.shape[0] - NOTE_ROWS:, :128].astype(jnp.float32)
        total = total + COUNT_BASE * notes[:1] + notes[1:2]
    return total


def load_keys(place, k_refs, v_refs, kband, vtband):
    for n, (k, v) in enumerate(zip(gathered(k_refs, place), gathered(v_refs, place))):
        rows = slice(n * k.shape[0], (n + 1) * k.shape[0])
        kband[rows] = k
        vtband[:HEAD_DIM, rows] = v.astype(jnp.float32).T.astype(vtband.dtype)
    vtband[HEAD_DIM:] = jnp.ones(vtband[HEAD_DIM:].shape, vtband.dtype)


def load_grads(place, half, k_refs, v_refs, part_refs, ktband, vband, dk_acc, dv_acc, dt_all):
    for n, (k, v) in enumerate(zip(gathered(k_refs, place), gathered(v_refs, place))):
        rows = slice(n * k.shape[0], (n + 1) * k.shape[0])
        ktband[:, rows] = k.astype(jnp.float32).T.astype(ktband.dtype)
        vband[rows] = v
    dk_acc[...] = jnp.zeros(dk_acc.shape, dk_acc.dtype)
    dv_acc[...] = jnp.zeros(dv_acc.shape, dv_acc.dtype)
    for n, part_ref in enumerate(part_refs):
        width = part_ref.shape[0] - NOTE_ROWS
        source = (place % half + half - n) % half
        part = part_ref[:width].astype(jnp.float32)
        for c in range(dt_all.shape[0]):
            dt_all[c, pl.ds(pl.multiple_of(source * width, 8), width)] = part[:, c * TILE:(c + 1) * TILE]


def slope_lanes(slope_ref, first, group):
    return jnp.concatenate([jnp.full((1, TILE), slope_ref[first + h] * LOG2E, jnp.float32) for h in range(group)], 1)


def load_bias(slope_row, bias):
    bias[...] = lax.broadcasted_iota(jnp.int32, bias.shape, 0).astype(jnp.float32) * slope_row


def soften(sub, place, reach, subs, slope_row, q, kband, vtband, bias, scores, e_ref):
    keys, lanes = scores.shape
    key_tiles = keys // TILE
    scale = LOG2E / math.sqrt(HEAD_DIM)
    qt = flipped_heads(q)
    below = (lax.broadcasted_iota(jnp.int32, (TILE, lanes), 0)
             > lax.broadcasted_iota(jnp.int32, (TILE, lanes), 1) % TILE)
    start = pl.multiple_of(sub * TILE, TILE)
    invalid = jnp.maximum(reach - place, 0) * subs
    peak = None
    shifts = []
    for t in range(key_tiles):
        k_tile = kband[pl.ds(start + t * TILE, TILE)]
        s = jnp.dot(k_tile, qt, preferred_element_type=jnp.float32) * scale + bias[...]
        if t == 0:
            s = jnp.where(below, s, FAR)
        elif t == key_tiles - 1:
            s = jnp.where(below, FAR, s)
        scores[t * TILE:(t + 1) * TILE] = s
        shift = slope_row * (t * TILE) + jnp.where(sub + t < invalid, FAR, 0.0)
        shifts.append(shift)
        top = jnp.max(s.reshape(TILE // 8, 8, lanes), 0) + shift
        peak = top if peak is None else jnp.maximum(peak, top)
    peak = jnp.max(peak, 0, keepdims=True)
    for t in range(key_tiles):
        e = jnp.exp2(scores[t * TILE:(t + 1) * TILE] - (peak - shifts[t]))
        e_ref[t * TILE:(t + 1) * TILE] = e.astype(e_ref.dtype)
    return jnp.dot(vtband[:, pl.ds(start, keys)], e_ref[...], preferred_element_type=jnp.float32)


def differentiate(sub, keep, q, o, e_ref, ktband, vband, dk_acc, dv_acc, ds_all, dt_all):
    keys, lanes = ds_all.shape
    start = pl.multiple_of(sub * TILE, TILE)
    keep = jnp.concatenate([keep] * (lanes // TILE), 1)
    inv = 1.0 / o[HEAD_DIM:HEAD_DIM + 1]
    dt = jnp.concatenate([dt_all[sub, n:n + HEAD_DIM] for n in range(0, lanes, TILE)], 1)
    dt = (dt * (keep * inv)).astype(jnp.bfloat16)
    d = flipped_heads(dt)
    delta = jnp.sum(dt.astype(jnp.float32) * o[:HEAD_DIM], 0, keepdims=True) * inv
    for t in range(keys // TILE):
        rows = pl.ds(start + t * TILE, TILE)
        e = e_ref[t * TILE:(t + 1) * TILE]
        dp = jnp.dot(vband[rows], dt, preferred_element_type=jnp.float32)
        ds = (e.astype(jnp.float32) * (dp - delta)).astype(jnp.bfloat16)
        ds_all[t * TILE:(t + 1) * TILE] = ds
        dv_acc[rows] += jnp.dot(e, d, preferred_element_type=jnp.float32)
        dk_acc[rows] += jnp.dot(ds, q, preferred_element_type=jnp.float32)
    return jnp.dot(ktband[:, pl.ds(start, keys)], ds_all[...], preferred_element_type=jnp.float32)


def store_sums(out_refs, dk_acc, dv_acc):
    for n, out_ref in enumerate(out_refs):
        rows = slice(n * out_ref.shape[0], (n + 1) * out_ref.shape[0])
        out_ref[:, :HEAD_DIM] = dk_acc[rows].astype(out_ref.dtype)
        out_ref[:, HEAD_DIM:] = dv_acc[rows].astype(out_ref.dtype)


def near_kernel(half, reach, place_ref, slope_ref, keep_ref, q_ref, k_refs, v_refs, part_refs,
                dqt_ref, far_two, far_one, own_ref, count_ref,
                kband, vtband, bias, scores, e_all, ktband, vband, dk_acc, dv_acc, ds_all, dt_all):
    place = place_ref[0]
    sub, subs = pl.program_id(0), pl.num_programs(0)
    group = scores.shape[1] // TILE
    slope_row = slope_lanes(slope_ref, head_of(place, half, True) * group, group)

    @pl.when(sub == 0)
    def _():
        load_keys(place, k_refs, v_refs, kband, vtband)
        load_bias(slope_row, bias)
        load_grads(place, half, k_refs, v_refs, part_refs, ktband, vband, dk_acc, dv_acc, dt_all)

    q = by_head(q_ref[...])
    o = soften(sub, place, reach, subs, slope_row, q, kband, vtband, bias, scores, e_all)
    dqt_ref[...] = differentiate(sub, keep_ref[...], q, o, e_all, ktband, vband, dk_acc, dv_acc, ds_all, dt_all)

    @pl.when(sub == subs - 1)
    def _():
        count_ref[...] = jnp.broadcast_to(counted(part_refs), count_ref.shape)
        store_sums((far_two, far_one, own_ref), dk_acc, dv_acc)


def prob_kernel(half, reach, place_ref, slope_ref, q_ref, k_refs, v_refs, e_ref, o_ref, kband, vtband, bias, scores):
    place = place_ref[0]
    sub, subs = pl.program_id(0), pl.num_programs(0)
    group = scores.shape[1] // TILE
    slope_row = slope_lanes(slope_ref, head_of(place, half, False) * group, group)

    @pl.when(sub == 0)
    def _():
        load_keys(place, k_refs, v_refs, kband, vtband)
        load_bias(slope_row, bias)

    o_ref[...] = soften(sub, place, reach, subs, slope_row, by_head(q_ref[...]), kband, vtband, bias, scores, e_ref)


def grad_kernel(half, seq_len, place_ref, distance_refs, keep_ref, q_ref, k_refs, v_refs, e_ref, o_ref, part_refs, near_dqt, count_ref,
                dq_ref, far_two, far_one, own_ref, weight_ref, ktband, vband, dk_acc, dv_acc, ds_all, dt_all):
    place = place_ref[0]
    sub = pl.program_id(0)
    lanes = ds_all.shape[1]

    @pl.when(sub == 0)
    def _():
        load_grads(place, half, k_refs, v_refs, part_refs, ktband, vband, dk_acc, dv_acc, dt_all)

    dqt = differentiate(sub, keep_ref[...], by_head(q_ref[...]), o_ref, e_ref, ktband, vband, dk_acc, dv_acc, ds_all,
                        dt_all)
    distance = [ref[:1].astype(jnp.float32) for ref in distance_refs]
    advantage = (sum(distance) * (1.0 / len(distance)) - distance[0]) * (1.0 / 64.0)
    weight = advantage * seq_len / (1.0 + count_ref[:1] + counted(part_refs))
    weight_ref[...] = jnp.broadcast_to(weight, weight_ref.shape)
    near = place // half
    for first, value in ((near * lanes, near_dqt[...]), ((1 - near) * lanes, dqt)):
        for n in range(0, lanes, TILE):
            cols = pl.ds(pl.multiple_of(first + n, TILE), TILE)
            dq_ref[:, cols] = (value[:, n:n + TILE].T * (weight * (1.0 / math.sqrt(HEAD_DIM)))).astype(dq_ref.dtype)

    @pl.when(sub == pl.num_programs(0) - 1)
    def _():
        store_sums((far_two, far_one, own_ref), dk_acc, dv_acc)


def returned_sums(place, half, total, back_refs, near):
    for n, back_ref in enumerate(back_refs):
        same = ((place + 1 + n) // half == place // half) == near
        back = back_ref[...].astype(jnp.float32)
        total = [total[0] + jnp.where(same, back, 0.0), total[1] + jnp.where(same, 0.0, back)]
    return total


def early_kernel(half, place_ref, own_near, own_other, back_refs, near_total, other_total):
    near_total[...], other_total[...] = returned_sums(
        place_ref[0], half, [own_near[...], own_other[...]], back_refs, True)


def final_kernel(half, place_ref, weight_ref, near_total, other_total, back_refs, dk_ref, dv_ref):
    place = place_ref[0]
    total = returned_sums(place, half, [near_total[...], other_total[...]], back_refs, False)
    high = place // half == 1
    total = [jnp.where(high, total[1], total[0]), jnp.where(high, total[0], total[1])]
    weight = weight_ref[:1, :HEAD_DIM]
    for n, value in enumerate(total):
        cols = slice(n * HEAD_DIM, (n + 1) * HEAD_DIM)
        dk_ref[:, cols] = (value[:, :HEAD_DIM] * (weight * (1.0 / math.sqrt(HEAD_DIM)))).astype(dk_ref.dtype)
        dv_ref[:, cols] = (value[:, HEAD_DIM:] * weight).astype(dv_ref.dtype)


def shards(query_rows, key_rows, value_rows, cotangent, slopes, lengths, loss_mask, distances):
    own_q = query_rows[0]
    own_k = key_rows[0]
    own_v = value_rows[0]
    tok_rows, features = own_q.shape
    kv_features = own_k.shape[1]
    head_count = features // HEAD_DIM
    kv_count = kv_features // HEAD_DIM
    group = head_count // kv_count
    reach = (WINDOW - 2) // tok_rows + 1
    band_len = (reach + 1) * tok_rows
    subs = tok_rows // TILE
    keys = WINDOW + TILE
    lanes = group * TILE
    o_rows = HEAD_DIM + 16
    n_seq = lax.axis_size("seq")
    n_roll = lax.axis_size("roll")
    seq_len = tok_rows * n_seq
    seq_pos = lax.axis_index("seq")
    half = n_seq // kv_count
    width = features // n_seq
    assert kv_count == 2 and width * half == lanes and reach == 2
    place = seq_pos[None].astype(jnp.int32)

    kv_pair = jnp.concatenate([own_k, own_v], 1)
    back_one = passed_along(kv_pair, "seq", 1)
    back_two_even = lax.ppermute(kv_pair, "seq", [(s, s + 2) for s in range(0, n_seq - 2, 2)])

    smem = pl.BlockSpec(memory_space=pltpu.SMEM)
    vmem = pl.BlockSpec(memory_space=pltpu.VMEM)
    params = pltpu.CompilerParams(vmem_limit_bytes=VMEM_LIMIT)
    piece = jax.ShapeDtypeStruct((width + NOTE_ROWS, tok_rows), jnp.bfloat16)
    keep, *pieces = pl.pallas_call(
        functools.partial(split_kernel, half),
        in_specs=[smem, smem, vmem, vmem],
        out_specs=[vmem] * (n_seq + 1),
        out_shape=[jax.ShapeDtypeStruct((1, tok_rows), jnp.float32)]
        + [piece] * n_seq,
        compiler_params=params,
        name="split_cotangent",
    )(place, lengths, cotangent[0].T, loss_mask)
    spread = jnp.broadcast_to(distances, (8, 128))
    apart = [spread]
    for shift in range(1, n_roll):
        apart.append(lax.ppermute(spread, "roll", [(n, (n + shift) % n_roll) for n in range(n_roll)]))
    pieces, back_one, apart = lax.optimization_barrier((pieces, back_one, apart))
    parts = {0: pieces[0]}
    for n in list(range(half, n_seq)) + list(range(1, half)):
        pairs = []
        for source in range(n_seq):
            side = source // half if n < half else 1 - source // half
            pairs.append((source, side * half + (source % half + n) % half))
        parts[n] = lax.ppermute(pieces[n], "seq", pairs)
    parts = [parts[n] for n in range(n_seq)]
    back_two_odd = lax.ppermute(back_one, "seq", [(s, s + 1) for s in range(2, n_seq, 2)])
    bands = [back_two_even, back_two_odd, back_one, kv_pair]

    pair_count = group * tok_rows * keys
    bf16, f32 = jnp.bfloat16, jnp.float32

    def head_specs(near, offset):
        spec = pl.BlockSpec((tok_rows, HEAD_DIM), lambda c, at: (0, offset + head_of(at[0], half, near)))
        return [spec] * len(bands)

    def q_spec(near):
        return pl.BlockSpec((TILE, lanes), lambda c, at: (c, head_of(at[0], half, near)))

    keep_spec = pl.BlockSpec((1, TILE), lambda c, at: (0, c))
    e_spec = pl.BlockSpec((None, keys, lanes), lambda c, at: (c, 0, 0))
    o_spec = pl.BlockSpec((None, o_rows, lanes), lambda c, at: (c, 0, 0))
    prob_scratch = [
        pltpu.VMEM((band_len, HEAD_DIM), bf16),
        pltpu.VMEM((o_rows, band_len), bf16),
        pltpu.VMEM((TILE, lanes), f32),
        pltpu.VMEM((keys, lanes), f32),
    ]
    grad_scratch = [
        pltpu.VMEM((HEAD_DIM, band_len), bf16),
        pltpu.VMEM((band_len, HEAD_DIM), bf16),
        pltpu.VMEM((band_len, HEAD_DIM), f32),
        pltpu.VMEM((band_len, HEAD_DIM), f32),
        pltpu.VMEM((keys, lanes), bf16),
        pltpu.VMEM((subs, lanes, TILE), f32),
    ]
    note = jax.ShapeDtypeStruct((8, 128), f32)
    dqt_spec = pl.BlockSpec((None, HEAD_DIM, lanes), lambda c, at: (c, 0, 0))
    grad_shapes = (
        jax.ShapeDtypeStruct((tok_rows, 2 * HEAD_DIM), bf16),
        jax.ShapeDtypeStruct((tok_rows, 2 * HEAD_DIM), bf16),
        jax.ShapeDtypeStruct((tok_rows, 2 * HEAD_DIM), f32),
    )

    def returned(sums):
        return [passed_along(sums[reach - offset], "seq", -offset) for offset in range(1, reach + 1)]

    e_all, o_all = pl.pallas_call(
        functools.partial(prob_kernel, half, reach),
        grid_spec=pltpu.PrefetchScalarGridSpec(
            num_scalar_prefetch=1,
            grid=(subs,),
            in_specs=[smem, q_spec(False), head_specs(False, 0), head_specs(False, kv_count)],
            out_specs=(e_spec, o_spec),
            scratch_shapes=prob_scratch,
        ),
        out_shape=(jax.ShapeDtypeStruct((subs, keys, lanes), bf16), jax.ShapeDtypeStruct((subs, o_rows, lanes), f32)),
        compiler_params=params,
        cost_estimate=pl.CostEstimate(flops=4 * pair_count * HEAD_DIM // COVER, transcendentals=0, bytes_accessed=1 << 16),
        name="other_probs",
    )(place, slopes, own_q, bands, bands)
    late_slopes, o_all = lax.optimization_barrier((slopes, o_all))
    near_dqt, *near_sums, near_count = pl.pallas_call(
        functools.partial(near_kernel, half, reach),
        grid_spec=pltpu.PrefetchScalarGridSpec(
            num_scalar_prefetch=1,
            grid=(subs,),
            in_specs=[smem, keep_spec, q_spec(True), head_specs(True, 0), head_specs(True, kv_count), [vmem] * half],
            out_specs=(dqt_spec, vmem, vmem, vmem, vmem),
            scratch_shapes=prob_scratch + [pltpu.VMEM((keys, lanes), bf16)] + grad_scratch,
        ),
        out_shape=(jax.ShapeDtypeStruct((subs, HEAD_DIM, lanes), f32),) + grad_shapes + (note,),
        compiler_params=params,
        cost_estimate=pl.CostEstimate(flops=12 * pair_count * HEAD_DIM // NEAR_COVER, transcendentals=0, bytes_accessed=1 << 16),
        name="near_head",
    )(place, late_slopes, keep, own_q, bands, bands, parts[:half])
    near_back = returned(near_sums)
    dq, *other_sums, weight = pl.pallas_call(
        functools.partial(grad_kernel, half, seq_len),
        grid_spec=pltpu.PrefetchScalarGridSpec(
            num_scalar_prefetch=1,
            grid=(subs,),
            in_specs=[[vmem] * n_roll, keep_spec, q_spec(False), head_specs(False, 0), head_specs(False, kv_count), e_spec, o_spec,
                      [vmem] * half, dqt_spec, vmem],
            out_specs=(pl.BlockSpec((TILE, features), lambda c, at: (c, 0)), vmem, vmem, vmem, vmem),
            scratch_shapes=grad_scratch,
        ),
        out_shape=(jax.ShapeDtypeStruct((tok_rows, features), bf16),) + grad_shapes + (note,),
        compiler_params=params,
        cost_estimate=pl.CostEstimate(flops=8 * pair_count * HEAD_DIM // COVER, transcendentals=0, bytes_accessed=1 << 16),
        name="other_grads",
    )(place, apart, keep, own_q, bands, bands, e_all, o_all, parts[half:], near_dqt, near_count)
    other_back = returned(other_sums)

    sums = jax.ShapeDtypeStruct((tok_rows, 2 * HEAD_DIM), f32)
    totals = pl.pallas_call(
        functools.partial(early_kernel, half),
        in_specs=[smem, vmem, vmem, [vmem] * reach],
        out_specs=(vmem, vmem),
        out_shape=(sums, sums),
        compiler_params=pltpu.CompilerParams(vmem_limit_bytes=8 << 20),
        name="sum_near",
    )(place, near_sums[-1], other_sums[-1], near_back)
    out = jax.ShapeDtypeStruct((tok_rows, kv_features), bf16)
    grad_k, grad_v = pl.pallas_call(
        functools.partial(final_kernel, half),
        in_specs=[smem, vmem, vmem, vmem, [vmem] * reach],
        out_specs=(vmem, vmem),
        out_shape=(out, out),
        compiler_params=pltpu.CompilerParams(vmem_limit_bytes=8 << 20),
        name="sum_other",
    )(place, weight, *totals, other_back)
    return (dq[None], grad_k[None], grad_v[None])


def solution(mesh):
    placed = (
        P("roll", "seq", None),
        P("roll", "seq", None),
        P("roll", "seq", None),
        P("roll", None, "seq"),
        P(),
        P("roll"),
        P("roll", "seq"),
        P("roll"),
    )
    return jax.shard_map(
        shards,
        mesh=mesh,
        in_specs=placed,
        out_specs=(P("roll", "seq", None), P("roll", "seq", None), P("roll", "seq", None)),
        check_vma=False,
    )
```
